128 devices in a mesh: seq: 32 (over z, x, core), head: 4 (over y).
Axes of the slice: x: 4, y: 4, z: 4, core: 2. Of those that a mesh axis runs over, the one named last changes fastest.
Arguments:
- inputs: bfloat16 [32768, 2048], P('seq', 'head'), may hold values from -6 to 6
- w_qkv: bfloat16 [3, 2048, 2048], P(None, None, 'head'), may hold values from -0.125 to 0.125
- level_weight: float32 [16, 6], P('head'), may hold values from 0.5 to 2
- grad_out: bfloat16 [32768, 2048], P('seq', 'head'), may hold values from -6 to 6
Outputs:
- attn_out: bfloat16 [32768, 2048], P('seq', 'head')
- grad_query: bfloat16 [32768, 2048], P('seq', 'head')
- grad_key: bfloat16 [32768, 2048], P('seq', 'head')
- grad_value: bfloat16 [32768, 2048], P('seq', 'head')
The draws below stay inside these ranges and needn't reach their ends.
All inputs are finite; a program needn't handle non-finite values.
Results may differ from the reference program's by a relative error of at most 0.012.
Values may be sent and summed in bfloat16 or wider, within the bound.
A program may use at most 128 MiB of HBM per device.

```python
import math
import jax
import jax.numpy as jnp
from jax import lax

D = 2048
H = 16
E = 128
TOK_DEV = 1024
TOKENS = 32768
LEVELS = 6
N_SEQ = 32


def levels(rng, dims, cuts, low, top_value):
    def one(position, parts):
        draws = jax.random.uniform(jax.random.fold_in(jax.random.fold_in(rng, 6), position), (parts,), jnp.float32, low / len(cuts), top_value / len(cuts))
        return jnp.repeat(jnp.exp(draws), dims[position] // parts).reshape((-1,) + (1,) * (len(dims) - position - 1))

    loudness = one(*cuts[0])
    for cut in cuts[1:]:
        loudness = loudness * one(*cut)
    return loudness


def normal_values(key, dims, deviation, limit, cuts=(), kind=jnp.bfloat16):
    result = jax.random.normal(key, dims, jnp.float32) * deviation
    if len(cuts) > 0:
        result = levels(key, dims, cuts, -0.22, 0.18) * result
    return jnp.clip(result, min=-limit, max=limit).astype(kind)


def setup_inputs(seed: int = 0) -> dict:
    key_of = jax.random.split(jax.random.key(seed), 5)
    return {
        "inputs": normal_values(key_of[0], (TOKENS, D), 1.0, 6.0, ((0, 32), (1, 4))),
        "w_qkv": normal_values(key_of[1], (3, D, H * E), D ** -0.5, 0.125, ((2, 4),)),
        "level_weight": jnp.clip(jnp.exp(math.log(2.0) - 1.3862944 * jax.random.uniform(key_of[2], (H, LEVELS), jnp.float32) ** levels(key_of[2], (H, LEVELS), ((0, 4),), -0.2, 0.2)), 0.5, 2.0),
        "grad_out": normal_values(key_of[3], (TOKENS, H * E), 1.0, 6.0, ((0, 32), (1, 4))),
    }


def reference(inputs, w_qkv, level_weight, grad_out):
    projected = [jnp.dot(inputs, w_qkv[j], preferred_element_type=jnp.float32).astype(jnp.bfloat16) for j in range(3)]
    queries = projected[0].reshape(N_SEQ, TOK_DEV, H, E)
    keys = projected[1].reshape(N_SEQ, TOK_DEV, H, E)
    values = projected[2].reshape(N_SEQ, TOK_DEV, H, E)
    grad_rows = grad_out.reshape(N_SEQ, TOK_DEV, H, E)
    key_state = jnp.einsum('cthd,cthe->chde', keys.astype(jnp.float32), values.astype(jnp.float32))
    query_state = jnp.einsum('cthd,cthe->chde', queries.astype(jnp.float32), grad_rows.astype(jnp.float32))
    forward_list = []
    backward_list = []
    for block in range(N_SEQ):
        forward_mix = jnp.zeros((H, E, E), jnp.float32)
        backward_mix = jnp.zeros((H, E, E), jnp.float32)
        for bit_level in range(LEVELS - 1):
            sibling_size = 2 ** bit_level
            parent_start = block >> bit_level + 1 << bit_level + 1
            level_scale = (level_weight[:, bit_level + 1] / math.sqrt(E * TOK_DEV * sibling_size))[:, None, None]
            if block >> bit_level & 1:
                forward_mix = forward_mix + level_scale * lax.optimization_barrier(jnp.sum(key_state[parent_start:parent_start + sibling_size], axis=0))
            else:
                backward_mix = backward_mix + level_scale * lax.optimization_barrier(jnp.sum(query_state[parent_start + sibling_size:parent_start + 2 * sibling_size], axis=0))
        forward_list.append(forward_mix.astype(jnp.bfloat16))
        backward_list.append(backward_mix.astype(jnp.bfloat16))
    forward_all = jnp.stack(forward_list)
    backward_all = jnp.stack(backward_list)
    local_scale = (level_weight[:, 0] / math.sqrt(E * TOK_DEV))[:, None, None]
    causal = jnp.arange(TOK_DEV)[:, None] >= jnp.arange(TOK_DEV)[None, :]

    def one_block(pieces):
        block_q, block_k, block_v, block_g, forward_mix, backward_mix = pieces
        query_f = block_q.astype(jnp.float32)
        key_f = block_k.astype(jnp.float32)
        value_f = block_v.astype(jnp.float32)
        grad_f = block_g.astype(jnp.float32)
        forward_f = forward_mix.astype(jnp.float32)
        backward_f = backward_mix.astype(jnp.float32)
        scores = jnp.einsum('thd,shd->hts', query_f, key_f)
        attend = jnp.where(causal[None], scores * local_scale, 0.0).astype(jnp.bfloat16)
        grad_scores = jnp.einsum('the,she->hts', grad_f, value_f)
        grad_attend = jnp.where(causal[None], grad_scores * local_scale, 0.0).astype(jnp.bfloat16)
        attend_f = attend.astype(jnp.float32)
        grad_attend_f = grad_attend.astype(jnp.float32)
        output = jnp.einsum('hts,she->the', attend_f, value_f) + jnp.einsum('thd,hde->the', query_f, forward_f)
        grad_q = jnp.einsum('hts,shd->thd', grad_attend_f, key_f) + jnp.einsum('the,hde->thd', grad_f, forward_f)
        grad_k = jnp.einsum('hts,thd->shd', grad_attend_f, query_f) + jnp.einsum('the,hde->thd', value_f, backward_f)
        grad_v = jnp.einsum('hts,the->she', attend_f, grad_f) + jnp.einsum('thd,hde->the', key_f, backward_f)
        return (output.astype(jnp.bfloat16), grad_q.astype(jnp.bfloat16), grad_k.astype(jnp.bfloat16), grad_v.astype(jnp.bfloat16))
    output, grad_q, grad_k, grad_v = lax.map(one_block, (queries, keys, values, grad_rows, forward_all, backward_all))
    return (output.reshape(TOKENS, H * E), grad_q.reshape(TOKENS, H * E), grad_k.reshape(TOKENS, H * E), grad_v.reshape(TOKENS, H * E))
```

```python
import functools
import math

import jax
import jax.numpy as jnp
from jax import lax
from jax.experimental import pallas as pl
from jax.experimental.pallas import tpu as pltpu
from jax.sharding import PartitionSpec as P

MESH = pl.DeviceIdType.MESH
NS = 32
NH = 4
ROWS = 1024
FEAT = 512
HEADS = 4
E = 128
STEPS = 8
ST = ROWS // STEPS
HALF = ST // 2
CHUNKS = 4
T = ROWS // CHUNKS
AHEAD = 4
FAR = 3 * FEAT
F32 = jnp.float32
BF16 = jnp.bfloat16


def dot(a, b):
    return jnp.dot(a, b, preferred_element_type=F32)


def dot_nt(a, b):
    return lax.dot_general(a, b, (((1,), (1,)), ((), ())), preferred_element_type=F32)


def dot_tn(a, b):
    return lax.dot_general(a, b, (((0,), (0,)), ((), ())), preferred_element_type=F32)


def main_kernel(
    x_ref, w_ref, lw_ref, g_ref,
    qkvg, acc, diag,
    xg, wv, pacc, kst, qst, sbuf, rbuf, mix, fbuf,
    own_s, own_r, rel_s, rel_r, loc_sem, w_sem, g_sem, s1, r1, s2, r2,
):
    me = lax.axis_index("seq")
    y = lax.axis_index("head")
    right = lax.rem(y + 1, NH)
    left = lax.rem(y + 3, NH)
    far = lax.rem(y + 2, NH)

    sources = (y, left, right, far)
    w_copies = [
        pltpu.make_async_copy(
            w_ref.at[:, pl.ds(pl.multiple_of(src * FEAT, FEAT), FEAT), :],
            wv.at[:, slot * FEAT : (slot + 1) * FEAT, :],
            w_sem.at[slot],
        )
        for slot, src in enumerate(sources)
    ]
    x_copy = pltpu.make_async_copy(x_ref, xg.at[:, 0:FEAT], loc_sem)
    g_copy = pltpu.make_async_copy(g_ref, qkvg.at[3], g_sem)

    barrier = pltpu.get_barrier_semaphore()
    for other in (left, right):
        pl.semaphore_signal(barrier, inc=1, device_id={"head": other}, device_id_type=MESH)

    def greet(d, c):
        pl.semaphore_signal(
            barrier, inc=1, device_id={"seq": lax.rem(me + d, NS)}, device_id_type=MESH
        )
        return c

    lax.fori_loop(1, NS, greet, 0)
    x_copy.start()
    for copy in w_copies:
        copy.start()
    g_copy.start()
    pl.semaphore_wait(barrier, NS + 1)

    def own(j, way, half):
        rows = pl.ds(pl.multiple_of(j * ST + half * HALF, HALF), HALF)
        return pltpu.make_async_remote_copy(
            src_ref=x_ref.at[rows, :],
            dst_ref=xg.at[rows, (way + 1) * FEAT : (way + 2) * FEAT],
            send_sem=own_s.at[j, way, half],
            recv_sem=own_r.at[j, way, half],
            device_id={"head": right if way == 0 else left},
            device_id_type=MESH,
        )

    def relay(j, way):
        rows = pl.ds(pl.multiple_of(j * ST + way * HALF, HALF), HALF)
        return pltpu.make_async_remote_copy(
            src_ref=xg.at[rows, (way + 1) * FEAT : (way + 2) * FEAT],
            dst_ref=xg.at[rows, FAR : FAR + FEAT],
            send_sem=rel_s.at[j, way],
            recv_sem=rel_r.at[j, way],
            device_id={"head": right if way == 0 else left},
            device_id_type=MESH,
        )

    def start_own(j):
        for half in range(2):
            own(j, 0, half).start()
            own(j, 1, 1 - half).start()

    for j in range(AHEAD):
        start_own(j)
    diag[...] = jnp.zeros_like(diag)
    kst[0] = jnp.zeros((FEAT, E), F32)
    qst[0] = jnp.zeros((FEAT, E), F32)
    x_copy.wait()
    for copy in w_copies:
        copy.wait()
    g_copy.wait()

    def poll(j):
        for way in range(2):
            own(j, way, way).wait_recv()
            relay(j, way).start()

        @pl.when(j + AHEAD < STEPS)
        def _():
            start_own(j + AHEAD)

        for way in range(2):
            own(j, way, 1 - way).wait_recv()

    def chunk_rows(i):
        return pl.ds(pl.multiple_of(i * T, T), T)

    def project_near(i):
        rows = chunk_rows(i)
        for p in range(3):
            pacc[p, rows, :] = dot(xg[rows, 0:FAR], wv[p, 0:FAR, :])

    def project_far(i):
        rows = chunk_rows(i)
        for step in range(2):
            for way in range(2):
                relay(2 * i + step, way).wait_recv()
        for p in range(3):
            full = pacc[p, rows, :] + dot(xg[rows, FAR : FAR + FEAT], wv[p, FAR : FAR + FEAT, :])
            qkvg[p, rows, :] = full.astype(BF16)
        for h in range(HEADS):
            cols = slice(h * E, (h + 1) * E)
            kst[i + 1, cols, :] = kst[i, cols, :] + dot_tn(qkvg[1, rows, cols], qkvg[2, rows, cols])
            qst[i + 1, cols, :] = qst[i, cols, :] + dot_tn(qkvg[0, rows, cols], qkvg[3, rows, cols])

    def local_scale(h):
        return lw_ref[h, 0] * (1.0 / math.sqrt(E * ROWS))

    def attend(i):
        rows = chunk_rows(i)
        at = lax.broadcasted_iota(jnp.int32, (T, T), 0)
        to = lax.broadcasted_iota(jnp.int32, (T, T), 1)
        for h in range(HEADS):
            cols = slice(h * E, (h + 1) * E)
            scale = local_scale(h)
            q, k, v, g = (qkvg[n, rows, cols] for n in range(4))
            before = (kst[i, cols, :] * scale).astype(BF16)
            low = at >= to
            up = at <= to
            a = jnp.where(low, dot_nt(q, k) * scale, 0.0).astype(BF16)
            acc[0, rows, cols] = dot(a, v) + dot(q, before)
            b = jnp.where(low, dot_nt(g, v) * scale, 0.0).astype(BF16)
            acc[1, rows, cols] = dot(b, k) + dot_nt(g, before)
            bt = jnp.where(up, dot_nt(v, g) * scale, 0.0).astype(BF16)
            acc[2, rows, cols] = dot(bt, q)
            a_t = jnp.where(up, dot_nt(k, q) * scale, 0.0).astype(BF16)
            acc[3, rows, cols] = dot(a_t, g)

    def chunk(i, c):
        poll(2 * i)
        poll(2 * i + 1)
        project_near(i)

        @pl.when(i >= 1)
        def _():
            project_far(i - 1)
            attend(i - 1)

        return c

    lax.fori_loop(0, CHUNKS, chunk, 0)
    project_far(CHUNKS - 1)

    sbuf[:, 0:16, :] = kst[CHUNKS].reshape(NS, 16, E).astype(BF16)
    sbuf[:, 16:32, :] = qst[CHUNKS].reshape(NS, 16, E).astype(BF16)

    def give(p):
        return pltpu.make_async_remote_copy(
            src_ref=sbuf.at[p], dst_ref=rbuf.at[me], send_sem=s1.at[p], recv_sem=r1.at[me],
            device_id={"seq": p}, device_id_type=MESH,
        )

    def take(p):
        return pltpu.make_async_remote_copy(
            src_ref=sbuf.at[p], dst_ref=rbuf.at[p], send_sem=s1.at[p], recv_sem=r1.at[p],
            device_id={"seq": p}, device_id_type=MESH,
        )

    def give_mix(p):
        return pltpu.make_async_remote_copy(
            src_ref=mix.at[p], dst_ref=fbuf.at[me], send_sem=s2.at[p], recv_sem=r2.at[me],
            device_id={"seq": p}, device_id_type=MESH,
        )

    def take_mix(p):
        return pltpu.make_async_remote_copy(
            src_ref=mix.at[p], dst_ref=fbuf.at[p], send_sem=s2.at[p], recv_sem=r2.at[p],
            device_id={"seq": p}, device_id_type=MESH,
        )

    def others(fn):
        def body(d, c):
            fn(lax.rem(me + d, NS))
            return c

        lax.fori_loop(1, NS, body, 0)

    others(lambda p: give(p).start())
    rbuf[me] = sbuf[me]

    attend(CHUNKS - 1)

    def later(i, c):
        rows = chunk_rows(i)
        for h in range(HEADS):
            cols = slice(h * E, (h + 1) * E)
            after = ((qst[CHUNKS, cols, :] - qst[i + 1, cols, :]) * local_scale(h)).astype(BF16)
            acc[2, rows, cols] += dot_nt(qkvg[2, rows, cols], after)
            acc[3, rows, cols] += dot(qkvg[1, rows, cols], after)
        return c

    lax.fori_loop(0, CHUNKS - 1, later, 0)

    others(lambda p: take(p).wait_recv())
    head = me // (NS // HEADS)
    coef = [lw_ref[head, b + 1] * (1.0 / math.sqrt(E * ROWS * 2**b)) for b in range(5)]
    for part in range(2):
        part_rows = slice(part * 16, part * 16 + 16)
        sums = [rbuf[c, part_rows, :].astype(F32) for c in range(NS)]
        total = [None] * NS
        for b in range(5):
            for c in range(NS):
                bit = c >> b & 1
                if bit == 1 - part:
                    term = coef[b] * sums[(c >> b) ^ 1]
                    total[c] = term if total[c] is None else total[c] + term
            sums = [sums[2 * n] + sums[2 * n + 1] for n in range(len(sums) // 2)]
        for c in range(NS):
            value = jnp.zeros((16, E), F32) if total[c] is None else total[c]
            mix[c, part_rows, :] = value.astype(BF16)
    others(lambda p: give_mix(p).start())
    fbuf[me] = mix[me]
    for j in range(STEPS):
        for way in range(2):
            relay(j, way).wait_send()
            for half in range(2):
                own(j, way, half).wait_send()
    others(lambda p: give(p).wait_send())
    others(lambda p: take_mix(p).wait_recv())
    for h in range(HEADS):
        pair, side = h // 2, h % 2
        span = slice(side * E, (side + 1) * E)
        for part in range(2):
            block = fbuf[8 * h : 8 * h + 8, part * 16 : part * 16 + 16, :].reshape(E, E)
            diag[part, pair, span, span] = block
    others(lambda p: give_mix(p).wait_send())


def finish_kernel(qkvg, acc, diag, o_ref, gq_ref, gk_ref, gv_ref, buf, sem):
    outs = (o_ref, gq_ref, gk_ref, gv_ref)
    plan = ((0, 0, dot), (3, 0, dot_nt), (2, 1, dot_nt), (1, 1, dot))
    copies = []
    for i in range(CHUNKS):
        rows = slice(i * T, (i + 1) * T)
        for n, (lhs, part, fn) in enumerate(plan):
            for pair in range(2):
                cols = slice(pair * 2 * E, (pair + 1) * 2 * E)
                value = acc[n, rows, cols] + fn(qkvg[lhs, rows, cols], diag[part, pair])
                buf[n, rows, cols] = value.astype(BF16)
            copy = pltpu.make_async_copy(buf.at[n, rows, :], outs[n].at[rows, :], sem.at[n, i])
            copy.start()
            copies.append(copy)
    for copy in copies:
        copy.wait()


def per_device(inputs, w_qkv, level_weight, grad_out):
    any_spec = pl.BlockSpec(memory_space=pl.ANY)
    vmem = pl.BlockSpec(memory_space=pltpu.VMEM)
    dma = pltpu.SemaphoreType.DMA
    qkvg, acc, diag = pl.pallas_call(
        main_kernel,
        out_shape=(
            pltpu.VMEM((4, ROWS, FEAT), BF16),
            pltpu.VMEM((4, ROWS, FEAT), F32),
            pltpu.VMEM((2, 2, 2 * E, 2 * E), BF16),
        ),
        in_specs=[any_spec, any_spec, pl.BlockSpec(memory_space=pltpu.SMEM), any_spec],
        out_specs=(vmem, vmem, vmem),
        scratch_shapes=[
            pltpu.VMEM((ROWS, 4 * FEAT), BF16),
            pltpu.VMEM((3, 4 * FEAT, FEAT), BF16),
            pltpu.VMEM((3, ROWS, FEAT), F32),
            pltpu.VMEM((CHUNKS + 1, FEAT, E), F32),
            pltpu.VMEM((CHUNKS + 1, FEAT, E), F32),
            pltpu.VMEM((NS, 32, E), BF16),
            pltpu.VMEM((NS, 32, E), BF16),
            pltpu.VMEM((NS, 32, E), BF16),
            pltpu.VMEM((NS, 32, E), BF16),
            dma((STEPS, 2, 2)),
            dma((STEPS, 2, 2)),
            dma((STEPS, 2)),
            dma((STEPS, 2)),
            dma(()),
            dma((4,)),
            dma(()),
            dma((NS,)),
            dma((NS,)),
            dma((NS,)),
            dma((NS,)),
        ],
        compiler_params=pltpu.CompilerParams(
            collective_id=0, has_side_effects=True, vmem_limit_bytes=36 * 2**20
        ),
        name="gather_and_mix",
    )(inputs, w_qkv, level_weight, grad_out)
    out = jax.ShapeDtypeStruct((ROWS, FEAT), BF16)
    return pl.pallas_call(
        finish_kernel,
        out_shape=(out, out, out, out),
        in_specs=[vmem, vmem, vmem],
        out_specs=(any_spec,) * 4,
        scratch_shapes=[pltpu.VMEM((4, ROWS, FEAT), BF16), dma((4, CHUNKS))],
        name="finish",
    )(qkvg, acc, diag)


def solution(mesh):
    in_specs = (P("seq", "head"), P(None, None, "head"), P("head", None), P("seq", "head"))
    out_specs = (P("seq", "head"), P("seq", "head"), P("seq", "head"), P("seq", "head"))
    return jax.shard_map(
        per_device, mesh=mesh, in_specs=in_specs, out_specs=out_specs, check_vma=False
    )
```

```python
import functools
import math

import jax
import jax.numpy as jnp
from jax import lax
from jax.experimental import pallas as pl
from jax.experimental.pallas import tpu as pltpu
from jax.sharding import PartitionSpec as P

MESH = pl.DeviceIdType.MESH
NS = 32
NH = 4
ROWS = 1024
FEAT = 512
HEADS = 4
E = 128
STEPS = 8
ST = ROWS // STEPS
HALF = ST // 2
CHUNKS = 4
T = ROWS // CHUNKS
AHEAD = 4
FAR = 3 * FEAT
F32 = jnp.float32
BF16 = jnp.bfloat16


def dot(a, b):
    return jnp.dot(a, b, preferred_element_type=F32)


def dot_nt(a, b):
    return lax.dot_general(a, b, (((1,), (1,)), ((), ())), preferred_element_type=F32)


def dot_tn(a, b):
    return lax.dot_general(a, b, (((0,), (0,)), ((), ())), preferred_element_type=F32)


def main_kernel(
    x_ref, w_ref, lw_hbm, g_ref,
    qkvg, acc, diag,
    xg, wv, pacc, kst, qst, sbuf, rbuf, mix, fbuf,
    own_s, own_r, rel_s, rel_r, loc_sem, w_sem, g_sem, s1, r1, s2, r2, lw_ref, lw_sem,
):
    me = lax.axis_index("seq")
    y = lax.axis_index("head")
    right = lax.rem(y + 1, NH)
    left = lax.rem(y + 3, NH)
    far = lax.rem(y + 2, NH)

    sources = (y, left, right, far)
    w_copies = [
        pltpu.make_async_copy(
            w_ref.at[:, pl.ds(pl.multiple_of(src * FEAT, FEAT), FEAT), :],
            wv.at[:, slot * FEAT : (slot + 1) * FEAT, :],
            w_sem.at[slot],
        )
        for slot, src in enumerate(sources)
    ]
    x_copy = pltpu.make_async_copy(x_ref, xg.at[:, 0:FEAT], loc_sem)
    g_copy = pltpu.make_async_copy(g_ref, qkvg.at[3], g_sem)
    lw_copy = pltpu.make_async_copy(lw_hbm, lw_ref, lw_sem)

    barrier = pltpu.get_barrier_semaphore()
    for other in (left, right):
        pl.semaphore_signal(barrier, inc=1, device_id={"head": other}, device_id_type=MESH)

    def greet(d, c):
        pl.semaphore_signal(
            barrier, inc=1, device_id={"seq": lax.rem(me + d, NS)}, device_id_type=MESH
        )
        return c

    lax.fori_loop(1, NS, greet, 0)
    x_copy.start()
    for copy in w_copies:
        copy.start()
    g_copy.start()
    lw_copy.start()
    pl.semaphore_wait(barrier, NS + 1)

    def own(j, way, half):
        rows = pl.ds(pl.multiple_of(j * ST + half * HALF, HALF), HALF)
        return pltpu.make_async_remote_copy(
            src_ref=x_ref.at[rows, :],
            dst_ref=xg.at[rows, (way + 1) * FEAT : (way + 2) * FEAT],
            send_sem=own_s.at[j, way, half],
            recv_sem=own_r.at[j, way, half],
            device_id={"head": right if way == 0 else left},
            device_id_type=MESH,
        )

    def relay(j, way):
        rows = pl.ds(pl.multiple_of(j * ST + way * HALF, HALF), HALF)
        return pltpu.make_async_remote_copy(
            src_ref=xg.at[rows, (way + 1) * FEAT : (way + 2) * FEAT],
            dst_ref=xg.at[rows, FAR : FAR + FEAT],
            send_sem=rel_s.at[j, way],
            recv_sem=rel_r.at[j, way],
            device_id={"head": right if way == 0 else left},
            device_id_type=MESH,
        )

    def start_own(j):
        for half in range(2):
            own(j, 0, half).start()
            own(j, 1, 1 - half).start()

    for j in range(AHEAD):
        start_own(j)
    diag[...] = jnp.zeros_like(diag)
    kst[0] = jnp.zeros((FEAT, E), F32)
    qst[0] = jnp.zeros((FEAT, E), F32)
    x_copy.wait()
    for copy in w_copies:
        copy.wait()
    g_copy.wait()
    lw_copy.wait()

    def poll(j):
        for way in range(2):
            own(j, way, way).wait_recv()
            relay(j, way).start()

        @pl.when(j + AHEAD < STEPS)
        def _():
            start_own(j + AHEAD)

        for way in range(2):
            own(j, way, 1 - way).wait_recv()

    def chunk_rows(i):
        return pl.ds(pl.multiple_of(i * T, T), T)

    def project_near(i):
        rows = chunk_rows(i)
        for p in range(3):
            pacc[p, rows, :] = dot(xg[rows, 0:FAR], wv[p, 0:FAR, :])

    def project_far(i):
        rows = chunk_rows(i)
        for step in range(2):
            for way in range(2):
                relay(2 * i + step, way).wait_recv()
        for p in range(3):
            full = pacc[p, rows, :] + dot(xg[rows, FAR : FAR + FEAT], wv[p, FAR : FAR + FEAT, :])
            qkvg[p, rows, :] = full.astype(BF16)
        for h in range(HEADS):
            cols = slice(h * E, (h + 1) * E)
            kst[i + 1, cols, :] = kst[i, cols, :] + dot_tn(qkvg[1, rows, cols], qkvg[2, rows, cols])
            qst[i + 1, cols, :] = qst[i, cols, :] + dot_tn(qkvg[0, rows, cols], qkvg[3, rows, cols])

    def local_scale(h):
        return lw_ref[h, 0] * (1.0 / math.sqrt(E * ROWS))

    def attend(i):
        rows = chunk_rows(i)
        at = lax.broadcasted_iota(jnp.int32, (T, T), 0)
        to = lax.broadcasted_iota(jnp.int32, (T, T), 1)
        for h in range(HEADS):
            cols = slice(h * E, (h + 1) * E)
            scale = local_scale(h)
            q, k, v, g = (qkvg[n, rows, cols] for n in range(4))
            before = (kst[i, cols, :] * scale).astype(BF16)
            low = at >= to
            up = at <= to
            a = jnp.where(low, dot_nt(q, k) * scale, 0.0).astype(BF16)
            acc[0, rows, cols] = dot(a, v) + dot(q, before)
            b = jnp.where(low, dot_nt(g, v) * scale, 0.0).astype(BF16)
            acc[1, rows, cols] = dot(b, k) + dot_nt(g, before)
            bt = jnp.where(up, dot_nt(v, g) * scale, 0.0).astype(BF16)
            acc[2, rows, cols] = dot(bt, q)
            a_t = jnp.where(up, dot_nt(k, q) * scale, 0.0).astype(BF16)
            acc[3, rows, cols] = dot(a_t, g)

    def chunk(i, c):
        poll(2 * i)
        poll(2 * i + 1)
        project_near(i)

        @pl.when(i >= 1)
        def _():
            project_far(i - 1)
            attend(i - 1)

        return c

    lax.fori_loop(0, CHUNKS, chunk, 0)
    project_far(CHUNKS - 1)

    sbuf[:, 0:16, :] = kst[CHUNKS].reshape(NS, 16, E).astype(BF16)
    sbuf[:, 16:32, :] = qst[CHUNKS].reshape(NS, 16, E).astype(BF16)

    def give(p):
        return pltpu.make_async_remote_copy(
            src_ref=sbuf.at[p], dst_ref=rbuf.at[me], send_sem=s1.at[p], recv_sem=r1.at[me],
            device_id={"seq": p}, device_id_type=MESH,
        )

    def take(p):
        return pltpu.make_async_remote_copy(
            src_ref=sbuf.at[p], dst_ref=rbuf.at[p], send_sem=s1.at[p], recv_sem=r1.at[p],
            device_id={"seq": p}, device_id_type=MESH,
        )

    def give_mix(p):
        return pltpu.make_async_remote_copy(
            src_ref=mix.at[p], dst_ref=fbuf.at[me], send_sem=s2.at[p], recv_sem=r2.at[me],
            device_id={"seq": p}, device_id_type=MESH,
        )

    def take_mix(p):
        return pltpu.make_async_remote_copy(
            src_ref=mix.at[p], dst_ref=fbuf.at[p], send_sem=s2.at[p], recv_sem=r2.at[p],
            device_id={"seq": p}, device_id_type=MESH,
        )

    def others(fn):
        def body(d, c):
            fn(lax.rem(me + d, NS))
            return c

        lax.fori_loop(1, NS, body, 0)

    others(lambda p: give(p).start())
    rbuf[me] = sbuf[me]

    attend(CHUNKS - 1)

    def later(i, c):
        rows = chunk_rows(i)
        for h in range(HEADS):
            cols = slice(h * E, (h + 1) * E)
            after = ((qst[CHUNKS, cols, :] - qst[i + 1, cols, :]) * local_scale(h)).astype(BF16)
            acc[2, rows, cols] += dot_nt(qkvg[2, rows, cols], after)
            acc[3, rows, cols] += dot(qkvg[1, rows, cols], after)
        return c

    lax.fori_loop(0, CHUNKS - 1, later, 0)

    others(lambda p: take(p).wait_recv())
    head = me // (NS // HEADS)
    coef = [lw_ref[head, b + 1] * (1.0 / math.sqrt(E * ROWS * 2**b)) for b in range(5)]
    for part in range(2):
        part_rows = slice(part * 16, part * 16 + 16)
        sums = [rbuf[c, part_rows, :].astype(F32) for c in range(NS)]
        total = [None] * NS
        for b in range(5):
            for c in range(NS):
                bit = c >> b & 1
                if bit == 1 - part:
                    term = coef[b] * sums[(c >> b) ^ 1]
                    total[c] = term if total[c] is None else total[c] + term
            sums = [sums[2 * n] + sums[2 * n + 1] for n in range(len(sums) // 2)]
        for c in range(NS):
            value = jnp.zeros((16, E), F32) if total[c] is None else total[c]
            mix[c, part_rows, :] = value.astype(BF16)
    others(lambda p: give_mix(p).start())
    fbuf[me] = mix[me]
    for j in range(STEPS):
        for way in range(2):
            relay(j, way).wait_send()
            for half in range(2):
                own(j, way, half).wait_send()
    others(lambda p: give(p).wait_send())
    others(lambda p: take_mix(p).wait_recv())
    for h in range(HEADS):
        pair, side = h // 2, h % 2
        span = slice(side * E, (side + 1) * E)
        for part in range(2):
            block = fbuf[8 * h : 8 * h + 8, part * 16 : part * 16 + 16, :].reshape(E, E)
            diag[part, pair, span, span] = block
    others(lambda p: give_mix(p).wait_send())


def finish_kernel(qkvg, acc, diag, o_ref, gq_ref, gk_ref, gv_ref, buf, sem):
    outs = (o_ref, gq_ref, gk_ref, gv_ref)
    plan = ((0, 0, dot), (3, 0, dot_nt), (2, 1, dot_nt), (1, 1, dot))
    copies = []
    for i in range(CHUNKS):
        rows = slice(i * T, (i + 1) * T)
        for n, (lhs, part, fn) in enumerate(plan):
            for pair in range(2):
                cols = slice(pair * 2 * E, (pair + 1) * 2 * E)
                value = acc[n, rows, cols] + fn(qkvg[lhs, rows, cols], diag[part, pair])
                buf[n, rows, cols] = value.astype(BF16)
            copy = pltpu.make_async_copy(buf.at[n, rows, :], outs[n].at[rows, :], sem.at[n, i])
            copy.start()
            copies.append(copy)
    for copy in copies:
        copy.wait()


def per_device(inputs, w_qkv, level_weight, grad_out):
    place = pltpu.with_memory_space_constraint
    any_spec = pl.BlockSpec(memory_space=pl.ANY)
    vmem = pl.BlockSpec(memory_space=pltpu.VMEM)
    dma = pltpu.SemaphoreType.DMA
    qkvg, acc, diag = pl.pallas_call(
        main_kernel,
        out_shape=(
            pltpu.VMEM((4, ROWS, FEAT), BF16),
            pltpu.VMEM((4, ROWS, FEAT), F32),
            pltpu.VMEM((2, 2, 2 * E, 2 * E), BF16),
        ),
        in_specs=[any_spec] * 4,
        out_specs=(vmem, vmem, vmem),
        scratch_shapes=[
            pltpu.VMEM((ROWS, 4 * FEAT), BF16),
            pltpu.VMEM((3, 4 * FEAT, FEAT), BF16),
            pltpu.VMEM((3, ROWS, FEAT), F32),
            pltpu.VMEM((CHUNKS + 1, FEAT, E), F32),
            pltpu.VMEM((CHUNKS + 1, FEAT, E), F32),
            pltpu.VMEM((NS, 32, E), BF16),
            pltpu.VMEM((NS, 32, E), BF16),
            pltpu.VMEM((NS, 32, E), BF16),
            pltpu.VMEM((NS, 32, E), BF16),
            dma((STEPS, 2, 2)),
            dma((STEPS, 2, 2)),
            dma((STEPS, 2)),
            dma((STEPS, 2)),
            dma(()),
            dma((4,)),
            dma(()),
            dma((NS,)),
            dma((NS,)),
            dma((NS,)),
            dma((NS,)),
            pltpu.SMEM((HEADS, 6), F32),
            dma(()),
        ],
        compiler_params=pltpu.CompilerParams(
            collective_id=0, has_side_effects=True, vmem_limit_bytes=36 * 2**20
        ),
        name="gather_and_mix",
    )(*(place(a, pltpu.MemorySpace.HBM) for a in (inputs, w_qkv, level_weight, grad_out)))
    out = jax.ShapeDtypeStruct((ROWS, FEAT), BF16)
    return pl.pallas_call(
        finish_kernel,
        out_shape=(out, out, out, out),
        in_specs=[vmem, vmem, vmem],
        out_specs=(any_spec,) * 4,
        scratch_shapes=[pltpu.VMEM((4, ROWS, FEAT), BF16), dma((4, CHUNKS))],
        compiler_params=pltpu.CompilerParams(vmem_limit_bytes=8 * 2**20),
        name="finish",
    )(*(place(a, pltpu.MemorySpace.VMEM) for a in (qkvg, acc, diag)))


def solution(mesh):
    in_specs = (P("seq", "head"), P(None, None, "head"), P("head", None), P("seq", "head"))
    out_specs = (P("seq", "head"), P("seq", "head"), P("seq", "head"), P("seq", "head"))
    return jax.shard_map(
        per_device, mesh=mesh, in_specs=in_specs, out_specs=out_specs, check_vma=False
    )
```

```python
import functools
import math

import jax
import jax.numpy as jnp
from jax import lax
from jax.experimental import pallas as pl
from jax.experimental.pallas import tpu as pltpu
from jax.sharding import PartitionSpec as P

MESH = pl.DeviceIdType.MESH
NS = 32
NH = 4
ROWS = 1024
FEAT = 512
HEADS = 4
E = 128
STEPS = 8
ST = ROWS // STEPS
HALF = ST // 2
CHUNKS = 4
T = ROWS // CHUNKS
AHEAD = 4
FAR = 3 * FEAT
F32 = jnp.float32
BF16 = jnp.bfloat16


def dot(a, b):
    return jnp.dot(a, b, preferred_element_type=F32)


def dot_nt(a, b):
    return lax.dot_general(a, b, (((1,), (1,)), ((), ())), preferred_element_type=F32)


def dot_tn(a, b):
    return lax.dot_general(a, b, (((0,), (0,)), ((), ())), preferred_element_type=F32)


def main_kernel(
    x_ref, w_ref, lw_hbm, g_ref,
    qkvg, acc, diag,
    xg, wv, pacc, kst, qst, sbuf, rbuf, mix, fbuf,
    own_s, own_r, rel_s, rel_r, loc_sem, w_sem, g_sem, s1, r1, s2, r2, lw_ref, lw_sem, word,
):
    me = lax.axis_index("seq")
    y = lax.axis_index("head")
    right = lax.rem(y + 1, NH)
    left = lax.rem(y + 3, NH)
    far = lax.rem(y + 2, NH)

    sources = (y, left, right, far)
    w_copies = [
        pltpu.make_async_copy(
            w_ref.at[:, pl.ds(pl.multiple_of(src * FEAT, FEAT), FEAT), :],
            wv.at[:, slot * FEAT : (slot + 1) * FEAT, :],
            w_sem.at[slot],
        )
        for slot, src in enumerate(sources)
    ]
    x_copy = pltpu.make_async_copy(x_ref, xg.at[:, 0:FEAT], loc_sem)
    g_copy = pltpu.make_async_copy(g_ref, qkvg.at[3], g_sem)
    lw_copy = pltpu.make_async_copy(lw_hbm, lw_ref, lw_sem)

    core = lax.rem(me, 2)
    along_x = lax.rem(me // 2, 4)
    along_z = me // 8

    def at_offset(dz, dx, dc):
        z = lax.rem(along_z + dz, 4) * 8
        x = lax.rem(along_x + dx, 4) * 2
        return z + x + (core if dc == 0 else 1 - core)

    x_peers = [at_offset(0, d, 0) for d in (1, 3)]
    z_peers = [at_offset(d, 0, 0) for d in (1, 3)]
    partner = at_offset(0, 0, 1)
    barrier = pltpu.get_barrier_semaphore()

    def signal(sem, axis, device):
        pl.semaphore_signal(sem, inc=1, device_id={axis: device}, device_id_type=MESH)

    for device in (left, right):
        signal(barrier, "head", device)
    for device in (*x_peers, *z_peers, partner):
        signal(barrier, "seq", device)
    x_copy.start()
    for copy in w_copies:
        copy.start()
    g_copy.start()
    lw_copy.start()
    pl.semaphore_wait(barrier, 7)

    def own(j, way, half):
        rows = pl.ds(pl.multiple_of(j * ST + half * HALF, HALF), HALF)
        return pltpu.make_async_remote_copy(
            src_ref=x_ref.at[rows, :],
            dst_ref=xg.at[rows, (way + 1) * FEAT : (way + 2) * FEAT],
            send_sem=own_s.at[j, way, half],
            recv_sem=own_r.at[j, way, half],
            device_id={"head": right if way == 0 else left},
            device_id_type=MESH,
        )

    def relay(j, way):
        rows = pl.ds(pl.multiple_of(j * ST + way * HALF, HALF), HALF)
        return pltpu.make_async_remote_copy(
            src_ref=xg.at[rows, (way + 1) * FEAT : (way + 2) * FEAT],
            dst_ref=xg.at[rows, FAR : FAR + FEAT],
            send_sem=rel_s.at[j, way],
            recv_sem=rel_r.at[j, way],
            device_id={"head": right if way == 0 else left},
            device_id_type=MESH,
        )

    def start_own(j):
        for half in range(2):
            own(j, 0, half).start()
            own(j, 1, 1 - half).start()

    for j in range(AHEAD):
        start_own(j)
    for n, peers in enumerate((x_peers, z_peers, z_peers, [partner])):
        for device in peers:
            signal(word.at[n], "seq", device)
        pl.semaphore_wait(word.at[n], len(peers))
    diag[...] = jnp.zeros_like(diag)
    kst[0] = jnp.zeros((FEAT, E), F32)
    qst[0] = jnp.zeros((FEAT, E), F32)
    x_copy.wait()
    for copy in w_copies:
        copy.wait()
    g_copy.wait()
    lw_copy.wait()

    def poll(j):
        for way in range(2):
            own(j, way, way).wait_recv()
            relay(j, way).start()

        @pl.when(j + AHEAD < STEPS)
        def _():
            start_own(j + AHEAD)

        for way in range(2):
            own(j, way, 1 - way).wait_recv()

    def chunk_rows(i):
        return pl.ds(pl.multiple_of(i * T, T), T)

    def project_near(i):
        rows = chunk_rows(i)
        for p in range(3):
            pacc[p, rows, :] = dot(xg[rows, 0:FAR], wv[p, 0:FAR, :])

    def project_far(i):
        rows = chunk_rows(i)
        for step in range(2):
            for way in range(2):
                relay(2 * i + step, way).wait_recv()
        for p in range(3):
            full = pacc[p, rows, :] + dot(xg[rows, FAR : FAR + FEAT], wv[p, FAR : FAR + FEAT, :])
            qkvg[p, rows, :] = full.astype(BF16)
        for h in range(HEADS):
            cols = slice(h * E, (h + 1) * E)
            kst[i + 1, cols, :] = kst[i, cols, :] + dot_tn(qkvg[1, rows, cols], qkvg[2, rows, cols])
            qst[i + 1, cols, :] = qst[i, cols, :] + dot_tn(qkvg[0, rows, cols], qkvg[3, rows, cols])

    def local_scale(h):
        return lw_ref[h, 0] * (1.0 / math.sqrt(E * ROWS))

    def attend(i):
        rows = chunk_rows(i)
        at = lax.broadcasted_iota(jnp.int32, (T, T), 0)
        to = lax.broadcasted_iota(jnp.int32, (T, T), 1)
        for h in range(HEADS):
            cols = slice(h * E, (h + 1) * E)
            scale = local_scale(h)
            q, k, v, g = (qkvg[n, rows, cols] for n in range(4))
            before = (kst[i, cols, :] * scale).astype(BF16)
            low = at >= to
            up = at <= to
            a = jnp.where(low, dot_nt(q, k) * scale, 0.0).astype(BF16)
            acc[0, rows, cols] = dot(a, v) + dot(q, before)
            b = jnp.where(low, dot_nt(g, v) * scale, 0.0).astype(BF16)
            acc[1, rows, cols] = dot(b, k) + dot_nt(g, before)
            bt = jnp.where(up, dot_nt(v, g) * scale, 0.0).astype(BF16)
            acc[2, rows, cols] = dot(bt, q)
            a_t = jnp.where(up, dot_nt(k, q) * scale, 0.0).astype(BF16)
            acc[3, rows, cols] = dot(a_t, g)

    def chunk(i, c):
        poll(2 * i)
        poll(2 * i + 1)
        project_near(i)

        @pl.when(i >= 1)
        def _():
            project_far(i - 1)
            attend(i - 1)

        return c

    lax.fori_loop(0, CHUNKS, chunk, 0)
    project_far(CHUNKS - 1)

    sbuf[:, 0:16, :] = kst[CHUNKS].reshape(NS, 16, E).astype(BF16)
    sbuf[:, 16:32, :] = qst[CHUNKS].reshape(NS, 16, E).astype(BF16)

    steps = sorted(
        ((dz, dx, dc) for dz in range(4) for dx in range(4) for dc in range(2)),
        key=lambda o: -min(o[0], 4 - o[0]) - min(o[1], 4 - o[1]) - o[2] / 2,
    )[:-1]
    peers = [at_offset(*step) for step in steps]
    gives = [
        pltpu.make_async_remote_copy(
            src_ref=sbuf.at[p], dst_ref=rbuf.at[me], send_sem=s1.at[n], recv_sem=r1.at[n],
            device_id={"seq": p}, device_id_type=MESH,
        )
        for n, p in enumerate(peers)
    ]
    give_mixes = [
        pltpu.make_async_remote_copy(
            src_ref=mix.at[p], dst_ref=fbuf.at[me], send_sem=s2.at[n], recv_sem=r2.at[n],
            device_id={"seq": p}, device_id_type=MESH,
        )
        for n, p in enumerate(peers)
    ]

    for copy in gives:
        copy.start()
    rbuf[me] = sbuf[me]

    attend(CHUNKS - 1)

    def later(i, c):
        rows = chunk_rows(i)
        for h in range(HEADS):
            cols = slice(h * E, (h + 1) * E)
            after = ((qst[CHUNKS, cols, :] - qst[i + 1, cols, :]) * local_scale(h)).astype(BF16)
            acc[2, rows, cols] += dot_nt(qkvg[2, rows, cols], after)
            acc[3, rows, cols] += dot(qkvg[1, rows, cols], after)
        return c

    lax.fori_loop(0, CHUNKS - 1, later, 0)

    for copy in gives:
        copy.wait_recv()
    head = me // (NS // HEADS)
    coef = [lw_ref[head, b + 1] * (1.0 / math.sqrt(E * ROWS * 2**b)) for b in range(5)]
    for part in range(2):
        part_rows = slice(part * 16, part * 16 + 16)
        sums = [rbuf[c, part_rows, :].astype(F32) for c in range(NS)]
        total = [None] * NS
        for b in range(5):
            for c in range(NS):
                bit = c >> b & 1
                if bit == 1 - part:
                    term = coef[b] * sums[(c >> b) ^ 1]
                    total[c] = term if total[c] is None else total[c] + term
            sums = [sums[2 * n] + sums[2 * n + 1] for n in range(len(sums) // 2)]
        for c in range(NS):
            value = jnp.zeros((16, E), F32) if total[c] is None else total[c]
            mix[c, part_rows, :] = value.astype(BF16)
    for copy in give_mixes:
        copy.start()
    fbuf[me] = mix[me]
    for j in range(STEPS):
        for way in range(2):
            relay(j, way).wait_send()
            for half in range(2):
                own(j, way, half).wait_send()
    for copy in gives:
        copy.wait_send()
    for copy in give_mixes:
        copy.wait_recv()
    for h in range(HEADS):
        pair, side = h // 2, h % 2
        span = slice(side * E, (side + 1) * E)
        for part in range(2):
            block = fbuf[8 * h : 8 * h + 8, part * 16 : part * 16 + 16, :].reshape(E, E)
            diag[part, pair, span, span] = block
    for copy in give_mixes:
        copy.wait_send()


def finish_kernel(qkvg, acc, diag, o_ref, gq_ref, gk_ref, gv_ref, buf, sem):
    outs = (o_ref, gq_ref, gk_ref, gv_ref)
    plan = ((0, 0, dot), (3, 0, dot_nt), (2, 1, dot_nt), (1, 1, dot))
    copies = []
    for i in range(CHUNKS):
        rows = slice(i * T, (i + 1) * T)
        for n, (lhs, part, fn) in enumerate(plan):
            for pair in range(2):
                cols = slice(pair * 2 * E, (pair + 1) * 2 * E)
                value = acc[n, rows, cols] + fn(qkvg[lhs, rows, cols], diag[part, pair])
                buf[n, rows, cols] = value.astype(BF16)
            copy = pltpu.make_async_copy(buf.at[n, rows, :], outs[n].at[rows, :], sem.at[n, i])
            copy.start()
            copies.append(copy)
    for copy in copies:
        copy.wait()


def per_device(inputs, w_qkv, level_weight, grad_out):
    place = pltpu.with_memory_space_constraint
    any_spec = pl.BlockSpec(memory_space=pl.ANY)
    vmem = pl.BlockSpec(memory_space=pltpu.VMEM)
    dma = pltpu.SemaphoreType.DMA
    qkvg, acc, diag = pl.pallas_call(
        main_kernel,
        out_shape=(
            pltpu.VMEM((4, ROWS, FEAT), BF16),
            pltpu.VMEM((4, ROWS, FEAT), F32),
            pltpu.VMEM((2, 2, 2 * E, 2 * E), BF16),
        ),
        in_specs=[any_spec] * 4,
        out_specs=(vmem, vmem, vmem),
        scratch_shapes=[
            pltpu.VMEM((ROWS, 4 * FEAT), BF16),
            pltpu.VMEM((3, 4 * FEAT, FEAT), BF16),
            pltpu.VMEM((3, ROWS, FEAT), F32),
            pltpu.VMEM((CHUNKS + 1, FEAT, E), F32),
            pltpu.VMEM((CHUNKS + 1, FEAT, E), F32),
            pltpu.VMEM((NS, 32, E), BF16),
            pltpu.VMEM((NS, 32, E), BF16),
            pltpu.VMEM((NS, 32, E), BF16),
            pltpu.VMEM((NS, 32, E), BF16),
            dma((STEPS, 2, 2)),
            dma((STEPS, 2, 2)),
            dma((STEPS, 2)),
            dma((STEPS, 2)),
            dma(()),
            dma((4,)),
            dma(()),
            dma((NS,)),
            dma((NS,)),
            dma((NS,)),
            dma((NS,)),
            pltpu.SMEM((HEADS, 6), F32),
            dma(()),
            pltpu.SemaphoreType.REGULAR((4,)),
        ],
        compiler_params=pltpu.CompilerParams(
            collective_id=0, has_side_effects=True, vmem_limit_bytes=36 * 2**20
        ),
        name="gather_and_mix",
    )(*(place(a, pltpu.MemorySpace.HBM) for a in (inputs, w_qkv, level_weight, grad_out)))
    out = jax.ShapeDtypeStruct((ROWS, FEAT), BF16)
    return pl.pallas_call(
        finish_kernel,
        out_shape=(out, out, out, out),
        in_specs=[vmem, vmem, vmem],
        out_specs=(any_spec,) * 4,
        scratch_shapes=[pltpu.VMEM((4, ROWS, FEAT), BF16), dma((4, CHUNKS))],
        compiler_params=pltpu.CompilerParams(vmem_limit_bytes=8 * 2**20),
        name="finish",
    )(*(place(a, pltpu.MemorySpace.VMEM) for a in (qkvg, acc, diag)))


def solution(mesh):
    in_specs = (P("seq", "head"), P(None, None, "head"), P("head", None), P("seq", "head"))
    out_specs = (P("seq", "head"), P("seq", "head"), P("seq", "head"), P("seq", "head"))
    return jax.shard_map(
        per_device, mesh=mesh, in_specs=in_specs, out_specs=out_specs, check_vma=False
    )
```

```python
import functools
import math

import jax
import jax.numpy as jnp
from jax import lax
from jax.experimental import pallas as pl
from jax.experimental.pallas import tpu as pltpu
from jax.sharding import PartitionSpec as P

MESH = pl.DeviceIdType.MESH
NS = 32
NH = 4
ROWS = 1024
FEAT = 512
HEADS = 4
E = 128
STEPS = 8
ST = ROWS // STEPS
HALF = ST // 2
CHUNKS = 4
T = ROWS // CHUNKS
AHEAD = 4
FAR = 3 * FEAT
CHIPS = NS // 2
SLICE = FEAT // CHIPS
F32 = jnp.float32
BF16 = jnp.bfloat16


def dot(a, b):
    return jnp.dot(a, b, preferred_element_type=F32)


def dot_nt(a, b):
    return lax.dot_general(a, b, (((1,), (1,)), ((), ())), preferred_element_type=F32)


def dot_tn(a, b):
    return lax.dot_general(a, b, (((0,), (0,)), ((), ())), preferred_element_type=F32)


def main_kernel(
    x_ref, w_ref, lw_hbm, g_ref,
    qkvg, acc, diag,
    xg, wv, pacc, kst, qst, sbuf, rbuf, mix, fbuf,
    own_s, own_r, rel_s, rel_r, loc_sem, w_sem, g_sem, s1, r1, s2, r2, lw_ref, lw_sem, word,
):
    me = lax.axis_index("seq")
    y = lax.axis_index("head")
    right = lax.rem(y + 1, NH)
    left = lax.rem(y + 3, NH)
    far = lax.rem(y + 2, NH)

    sources = (y, left, right, far)
    w_copies = [
        pltpu.make_async_copy(
            w_ref.at[:, pl.ds(pl.multiple_of(src * FEAT, FEAT), FEAT), :],
            wv.at[:, slot * FEAT : (slot + 1) * FEAT, :],
            w_sem.at[slot],
        )
        for slot, src in enumerate(sources)
    ]
    x_copy = pltpu.make_async_copy(x_ref, xg.at[:, 0:FEAT], loc_sem)
    g_copy = pltpu.make_async_copy(g_ref, qkvg.at[3], g_sem)
    lw_copy = pltpu.make_async_copy(lw_hbm, lw_ref, lw_sem)

    core = lax.rem(me, 2)
    along_x = lax.rem(me // 2, 4)
    along_z = me // 8

    def at_offset(dz, dx, dc):
        z = lax.rem(along_z + dz, 4) * 8
        x = lax.rem(along_x + dx, 4) * 2
        return z + x + (core if dc == 0 else 1 - core)

    x_peers = [at_offset(0, d, 0) for d in (1, 3)]
    z_peers = [at_offset(d, 0, 0) for d in (1, 3)]
    partner = at_offset(0, 0, 1)
    barrier = pltpu.get_barrier_semaphore()

    def signal(sem, axis, device):
        pl.semaphore_signal(sem, inc=1, device_id={axis: device}, device_id_type=MESH)

    for device in (left, right):
        signal(barrier, "head", device)
    for device in (*x_peers, *z_peers, partner):
        signal(barrier, "seq", device)
    x_copy.start()
    for copy in w_copies:
        copy.start()
    g_copy.start()
    lw_copy.start()
    pl.semaphore_wait(barrier, 7)

    def own(j, way, half):
        rows = pl.ds(pl.multiple_of(j * ST + half * HALF, HALF), HALF)
        return pltpu.make_async_remote_copy(
            src_ref=x_ref.at[rows, :],
            dst_ref=xg.at[rows, (way + 1) * FEAT : (way + 2) * FEAT],
            send_sem=own_s.at[j, way, half],
            recv_sem=own_r.at[j, way, half],
            device_id={"head": right if way == 0 else left},
            device_id_type=MESH,
        )

    def relay(j, way):
        rows = pl.ds(pl.multiple_of(j * ST + way * HALF, HALF), HALF)
        return pltpu.make_async_remote_copy(
            src_ref=xg.at[rows, (way + 1) * FEAT : (way + 2) * FEAT],
            dst_ref=xg.at[rows, FAR : FAR + FEAT],
            send_sem=rel_s.at[j, way],
            recv_sem=rel_r.at[j, way],
            device_id={"head": right if way == 0 else left},
            device_id_type=MESH,
        )

    def start_own(j):
        for half in range(2):
            own(j, 0, half).start()
            own(j, 1, 1 - half).start()

    for j in range(AHEAD):
        start_own(j)
    for n, peers in enumerate((x_peers, z_peers, z_peers, [partner])):
        for device in peers:
            signal(word.at[n], "seq", device)
        pl.semaphore_wait(word.at[n], len(peers))
    diag[...] = jnp.zeros_like(diag)
    kst[0] = jnp.zeros((FEAT, E), F32)
    qst[0] = jnp.zeros((FEAT, E), F32)
    x_copy.wait()
    for copy in w_copies:
        copy.wait()
    g_copy.wait()
    lw_copy.wait()

    def poll(j):
        for way in range(2):
            own(j, way, way).wait_recv()
            relay(j, way).start()

        @pl.when(j + AHEAD < STEPS)
        def _():
            start_own(j + AHEAD)

        for way in range(2):
            own(j, way, 1 - way).wait_recv()

    def chunk_rows(i):
        return pl.ds(pl.multiple_of(i * T, T), T)

    def project_near(i):
        rows = chunk_rows(i)
        for p in range(3):
            pacc[p, rows, :] = dot(xg[rows, 0:FAR], wv[p, 0:FAR, :])

    def project_far(i):
        for h in range(HEADS):
            cols = slice(h * E, (h + 1) * E)
            kst[i + 1, cols, :] = kst[i, cols, :]
            qst[i + 1, cols, :] = qst[i, cols, :]
        far_step(i, 0)

        @pl.when(i < CHUNKS - 1)
        def _():
            far_step(i, 1)

    def far_step(i, step):
        rows = pl.ds(pl.multiple_of(i * T + step * ST, ST), ST)
        for way in range(2):
            relay(2 * i + step, way).wait_recv()
        project(rows, (0, 1, 2))
        add_states(i, rows, kst, 1, 2)
        add_states(i, rows, qst, 0, 3)

    def project(rows, parts):
        for p in parts:
            full = pacc[p, rows, :] + dot(xg[rows, FAR : FAR + FEAT], wv[p, FAR : FAR + FEAT, :])
            qkvg[p, rows, :] = full.astype(BF16)

    def add_states(i, rows, states, a, b):
        for h in range(HEADS):
            cols = slice(h * E, (h + 1) * E)
            states[i + 1, cols, :] += dot_tn(qkvg[a, rows, cols], qkvg[b, rows, cols])

    def local_scale(h):
        return lw_ref[h, 0] * (1.0 / math.sqrt(E * ROWS))

    def attend(i):
        rows = chunk_rows(i)
        at = lax.broadcasted_iota(jnp.int32, (T, T), 0)
        to = lax.broadcasted_iota(jnp.int32, (T, T), 1)
        for h in range(HEADS):
            cols = slice(h * E, (h + 1) * E)
            scale = local_scale(h)
            q, k, v, g = (qkvg[n, rows, cols] for n in range(4))
            before = (kst[i, cols, :] * scale).astype(BF16)
            low = at >= to
            up = at <= to
            a = jnp.where(low, dot_nt(q, k) * scale, 0.0).astype(BF16)
            acc[0, rows, cols] = dot(a, v) + dot(q, before)
            b = jnp.where(low, dot_nt(g, v) * scale, 0.0).astype(BF16)
            acc[1, rows, cols] = dot(b, k) + dot_nt(g, before)
            bt = jnp.where(up, dot_nt(v, g) * scale, 0.0).astype(BF16)
            acc[2, rows, cols] = dot(bt, q)
            a_t = jnp.where(up, dot_nt(k, q) * scale, 0.0).astype(BF16)
            acc[3, rows, cols] = dot(a_t, g)

    def chunk(i, c):
        poll(2 * i)
        poll(2 * i + 1)
        project_near(i)

        @pl.when(i >= 1)
        def _():
            project_far(i - 1)
            attend(i - 1)

        return c

    lax.fori_loop(0, CHUNKS, chunk, 0)
    project_far(CHUNKS - 1)

    chip = me // 2
    offsets = sorted(
        ((dz, dx, dc) for dz in range(4) for dx in range(4) for dc in range(2)),
        key=lambda o: (-o[2], -min(o[0], 4 - o[0]) - min(o[1], 4 - o[1])),
    )[:-1]
    peers = [at_offset(*offset) for offset in offsets]
    gives = []
    give_mixes = []
    for n, (offset, peer) in enumerate(zip(offsets, peers)):
        owned = core if offset[2] == 0 else 1 - core
        gives.append(
            pltpu.make_async_remote_copy(
                src_ref=sbuf.at[owned, peer // 2], dst_ref=rbuf.at[me],
                send_sem=s1.at[n], recv_sem=r1.at[n],
                device_id={"seq": peer}, device_id_type=MESH,
            )
        )
        give_mixes.append(
            pltpu.make_async_remote_copy(
                src_ref=mix.at[peer], dst_ref=fbuf.at[core, chip],
                send_sem=s2.at[n], recv_sem=r2.at[n],
                device_id={"seq": peer}, device_id_type=MESH,
            )
        )

    last = slice(ROWS - ST, ROWS)
    for way in range(2):
        relay(STEPS - 1, way).wait_recv()

    def last_step(kind, states, a, b, parts):
        project(last, parts)
        add_states(CHUNKS - 1, last, states, a, b)
        sbuf[kind] = states[CHUNKS].reshape(CHIPS, SLICE, E).astype(BF16)

    keys = (0, kst, 1, 2, (1, 2))
    queries = (1, qst, 0, 3, (0,))
    for n in range(2):

        @pl.when(core == 1 - n)
        def _():
            last_step(*keys)

        @pl.when(core == n)
        def _():
            last_step(*queries)

        for copy in gives[n * CHIPS : (n + 1) * CHIPS]:
            copy.start()
    rbuf[me] = sbuf[core, chip]

    attend(CHUNKS - 1)

    def later(i, c):
        rows = chunk_rows(i)
        for h in range(HEADS):
            cols = slice(h * E, (h + 1) * E)
            after = ((qst[CHUNKS, cols, :] - qst[i + 1, cols, :]) * local_scale(h)).astype(BF16)
            acc[2, rows, cols] += dot_nt(qkvg[2, rows, cols], after)
            acc[3, rows, cols] += dot(qkvg[1, rows, cols], after)
        return c

    lax.fori_loop(0, CHUNKS - 1, later, 0)

    for copy in gives:
        copy.wait_recv()
    def place_of(c):
        return c + core * (NS - 1 - 2 * c)

    head = chip // (CHIPS // HEADS)
    sums = [rbuf[place_of(c)].astype(F32) for c in range(NS)]
    total = [jnp.zeros((SLICE, E), F32)] * NS
    for b in range(5):
        coef = lw_ref[head, b + 1] * (1.0 / math.sqrt(E * ROWS * 2**b))
        for c in range(NS):
            if c >> b & 1:
                total[c] = total[c] + coef * sums[(c >> b) ^ 1]
        sums = [sums[2 * n] + sums[2 * n + 1] for n in range(len(sums) // 2)]
    for c in range(NS):
        mix[place_of(c)] = total[c].astype(BF16)
    for copy in give_mixes:
        copy.start()
    fbuf[core, chip] = mix[me]
    for j in range(STEPS):
        for way in range(2):
            relay(j, way).wait_send()
            for half in range(2):
                own(j, way, half).wait_send()
    for copy in gives:
        copy.wait_send()
    for copy in give_mixes:
        copy.wait_recv()

    per_head = CHIPS // HEADS
    for h in range(HEADS):
        pair, side = h // 2, h % 2
        span = slice(side * E, (side + 1) * E)
        for part in range(2):
            block = fbuf[part, h * per_head : (h + 1) * per_head].reshape(E, E)
            diag[part, pair, span, span] = block
    for copy in give_mixes:
        copy.wait_send()


def finish_kernel(qkvg, acc, diag, o_ref, gq_ref, gk_ref, gv_ref, buf, sem):
    outs = (o_ref, gq_ref, gk_ref, gv_ref)
    plan = ((0, 0, dot), (3, 0, dot_nt), (2, 1, dot_nt), (1, 1, dot))
    copies = []
    for i in range(CHUNKS):
        rows = slice(i * T, (i + 1) * T)
        for n, (lhs, part, fn) in enumerate(plan):
            for pair in range(2):
                cols = slice(pair * 2 * E, (pair + 1) * 2 * E)
                value = acc[n, rows, cols] + fn(qkvg[lhs, rows, cols], diag[part, pair])
                buf[n, rows, cols] = value.astype(BF16)
            copy = pltpu.make_async_copy(buf.at[n, rows, :], outs[n].at[rows, :], sem.at[n, i])
            copy.start()
            copies.append(copy)
    for copy in copies:
        copy.wait()


def per_device(inputs, w_qkv, level_weight, grad_out):
    place = pltpu.with_memory_space_constraint
    any_spec = pl.BlockSpec(memory_space=pl.ANY)
    vmem = pl.BlockSpec(memory_space=pltpu.VMEM)
    dma = pltpu.SemaphoreType.DMA
    state = pl.pallas_call(
        main_kernel,
        out_shape=(
            pltpu.VMEM((4, ROWS, FEAT), BF16),
            pltpu.VMEM((4, ROWS, FEAT), F32),
            pltpu.VMEM((2, 2, 2 * E, 2 * E), BF16),
        ),
        in_specs=[any_spec] * 4,
        out_specs=(vmem,) * 3,
        scratch_shapes=[
            pltpu.VMEM((ROWS, 4 * FEAT), BF16),
            pltpu.VMEM((3, 4 * FEAT, FEAT), BF16),
            pltpu.VMEM((3, ROWS, FEAT), F32),
            pltpu.VMEM((CHUNKS + 1, FEAT, E), F32),
            pltpu.VMEM((CHUNKS + 1, FEAT, E), F32),
            pltpu.VMEM((2, CHIPS, SLICE, E), BF16),
            pltpu.VMEM((NS, SLICE, E), BF16),
            pltpu.VMEM((NS, SLICE, E), BF16),
            pltpu.VMEM((2, CHIPS, SLICE, E), BF16),
            dma((STEPS, 2, 2)),
            dma((STEPS, 2, 2)),
            dma((STEPS, 2)),
            dma((STEPS, 2)),
            dma(()),
            dma((4,)),
            dma(()),
            dma((NS,)),
            dma((NS,)),
            dma((NS,)),
            dma((NS,)),
            pltpu.SMEM((HEADS, 6), F32),
            dma(()),
            pltpu.SemaphoreType.REGULAR((4,)),
        ],
        compiler_params=pltpu.CompilerParams(
            collective_id=0, has_side_effects=True, vmem_limit_bytes=36 * 2**20
        ),
        name="gather_and_mix",
    )(*(place(a, pltpu.MemorySpace.HBM) for a in (inputs, w_qkv, level_weight, grad_out)))
    out = jax.ShapeDtypeStruct((ROWS, FEAT), BF16)
    return pl.pallas_call(
        finish_kernel,
        out_shape=(out, out, out, out),
        in_specs=[vmem] * 3,
        out_specs=(any_spec,) * 4,
        scratch_shapes=[pltpu.VMEM((4, ROWS, FEAT), BF16), dma((4, CHUNKS))],
        compiler_params=pltpu.CompilerParams(vmem_limit_bytes=8 * 2**20),
        name="finish",
    )(*(place(a, pltpu.MemorySpace.VMEM) for a in state))


def solution(mesh):
    in_specs = (P("seq", "head"), P(None, None, "head"), P("head", None), P("seq", "head"))
    out_specs = (P("seq", "head"), P("seq", "head"), P("seq", "head"), P("seq", "head"))
    return jax.shard_map(
        per_device, mesh=mesh, in_specs=in_specs, out_specs=out_specs, check_vma=False
    )
```

```python
import functools
import math

import jax
import jax.numpy as jnp
from jax import lax
from jax.experimental import pallas as pl
from jax.experimental.pallas import tpu as pltpu
from jax.sharding import PartitionSpec as P

MESH = pl.DeviceIdType.MESH
NS = 32
NH = 4
ROWS = 1024
FEAT = 512
HEADS = 4
E = 128
STEPS = 8
ST = ROWS // STEPS
HALF = ST // 2
CHUNKS = 4
T = ROWS // CHUNKS
AHEAD = 2
FAR = 3 * FEAT
CHIPS = NS // 2
SLICE = FEAT // CHIPS
F32 = jnp.float32
BF16 = jnp.bfloat16


def dot(a, b):
    return jnp.dot(a, b, preferred_element_type=F32)


def dot_nt(a, b):
    return lax.dot_general(a, b, (((1,), (1,)), ((), ())), preferred_element_type=F32)


def dot_tn(a, b):
    return lax.dot_general(a, b, (((0,), (0,)), ((), ())), preferred_element_type=F32)


def main_kernel(
    x_ref, w_ref, lw_hbm, g_ref,
    qkvg, acc, diag,
    xg, wv, pacc, kst, qst, sbuf, rbuf, mix, fbuf,
    own_s, own_r, rel_s, rel_r, loc_sem, w_sem, g_sem, s1, r1, s2, r2, lw_ref, lw_sem, word,
):
    me = lax.axis_index("seq")
    y = lax.axis_index("head")
    right = lax.rem(y + 1, NH)
    left = lax.rem(y + 3, NH)
    far = lax.rem(y + 2, NH)

    sources = (y, left, right, far)
    w_copies = [
        pltpu.make_async_copy(
            w_ref.at[:, pl.ds(pl.multiple_of(src * FEAT, FEAT), FEAT), :],
            wv.at[:, slot * FEAT : (slot + 1) * FEAT, :],
            w_sem.at[slot],
        )
        for slot, src in enumerate(sources)
    ]
    x_copy = pltpu.make_async_copy(x_ref, xg.at[:, 0:FEAT], loc_sem)
    g_copy = pltpu.make_async_copy(g_ref, qkvg.at[3], g_sem)
    lw_copy = pltpu.make_async_copy(lw_hbm, lw_ref, lw_sem)

    core = lax.rem(me, 2)
    along_x = lax.rem(me // 2, 4)
    along_z = me // 8

    def at_offset(dz, dx, dc):
        z = lax.rem(along_z + dz, 4) * 8
        x = lax.rem(along_x + dx, 4) * 2
        return z + x + (core if dc == 0 else 1 - core)

    x_peers = [at_offset(0, d, 0) for d in (1, 3)]
    z_peers = [at_offset(d, 0, 0) for d in (1, 3)]
    partner = at_offset(0, 0, 1)
    barrier = pltpu.get_barrier_semaphore()

    def signal(sem, axis, device):
        pl.semaphore_signal(sem, inc=1, device_id={axis: device}, device_id_type=MESH)

    for device in (left, right):
        signal(barrier, "head", device)
    for device in (*x_peers, *z_peers, partner):
        signal(barrier, "seq", device)
    x_copy.start()
    for copy in w_copies:
        copy.start()
    g_copy.start()
    lw_copy.start()
    pl.semaphore_wait(barrier, 7)

    def own(i, way):
        rows = pl.ds(pl.multiple_of(i * T, T), T)
        return pltpu.make_async_remote_copy(
            src_ref=x_ref.at[rows, :],
            dst_ref=xg.at[rows, (way + 1) * FEAT : (way + 2) * FEAT],
            send_sem=own_s.at[i, way],
            recv_sem=own_r.at[i, way],
            device_id={"head": right if way == 0 else left},
            device_id_type=MESH,
        )

    def relay(j, way):
        rows = pl.ds(pl.multiple_of(j * ST + way * HALF, HALF), HALF)
        return pltpu.make_async_remote_copy(
            src_ref=xg.at[rows, (way + 1) * FEAT : (way + 2) * FEAT],
            dst_ref=xg.at[rows, FAR : FAR + FEAT],
            send_sem=rel_s.at[j, way],
            recv_sem=rel_r.at[j, way],
            device_id={"head": right if way == 0 else left},
            device_id_type=MESH,
        )

    def start_own(i):
        for way in range(2):
            own(i, way).start()

    for i in range(AHEAD):
        start_own(i)
    for n, peers in enumerate((x_peers, z_peers, z_peers, [partner])):
        for device in peers:
            signal(word.at[n], "seq", device)
        pl.semaphore_wait(word.at[n], len(peers))
    diag[...] = jnp.zeros_like(diag)
    kst[0] = jnp.zeros((FEAT, E), F32)
    qst[0] = jnp.zeros((FEAT, E), F32)
    x_copy.wait()
    for copy in w_copies:
        copy.wait()
    g_copy.wait()
    lw_copy.wait()

    def poll(i):
        for way in range(2):
            own(i, way).wait_recv()
            for step in range(T // ST):
                relay(i * (T // ST) + step, way).start()

        @pl.when(i + AHEAD < CHUNKS)
        def _():
            start_own(i + AHEAD)

    def chunk_rows(i):
        return pl.ds(pl.multiple_of(i * T, T), T)

    def project_near(i):
        rows = chunk_rows(i)
        for p in range(3):
            pacc[p, rows, :] = dot(xg[rows, 0:FAR], wv[p, 0:FAR, :])

    def project_far(i):
        for h in range(HEADS):
            cols = slice(h * E, (h + 1) * E)
            kst[i + 1, cols, :] = kst[i, cols, :]
            qst[i + 1, cols, :] = qst[i, cols, :]
        far_step(i, 0)

        @pl.when(i < CHUNKS - 1)
        def _():
            far_step(i, 1)

    def far_step(i, step):
        rows = pl.ds(pl.multiple_of(i * T + step * ST, ST), ST)
        for way in range(2):
            relay(2 * i + step, way).wait_recv()
        project(rows, (0, 1, 2))
        add_states(i, rows, kst, 1, 2)
        add_states(i, rows, qst, 0, 3)

    def project(rows, parts):
        for p in parts:
            full = pacc[p, rows, :] + dot(xg[rows, FAR : FAR + FEAT], wv[p, FAR : FAR + FEAT, :])
            qkvg[p, rows, :] = full.astype(BF16)

    def add_states(i, rows, states, a, b):
        for h in range(HEADS):
            cols = slice(h * E, (h + 1) * E)
            states[i + 1, cols, :] += dot_tn(qkvg[a, rows, cols], qkvg[b, rows, cols])

    def local_scale(h):
        return lw_ref[h, 0] * (1.0 / math.sqrt(E * ROWS))

    def attend(i):
        rows = chunk_rows(i)
        at = lax.broadcasted_iota(jnp.int32, (T, T), 0)
        to = lax.broadcasted_iota(jnp.int32, (T, T), 1)
        for h in range(HEADS):
            cols = slice(h * E, (h + 1) * E)
            scale = local_scale(h)
            q, k, v, g = (qkvg[n, rows, cols] for n in range(4))
            before = (kst[i, cols, :] * scale).astype(BF16)
            low = at >= to
            up = at <= to
            a = jnp.where(low, dot_nt(q, k) * scale, 0.0).astype(BF16)
            acc[0, rows, cols] = dot(a, v) + dot(q, before)
            b = jnp.where(low, dot_nt(g, v) * scale, 0.0).astype(BF16)
            acc[1, rows, cols] = dot(b, k) + dot_nt(g, before)
            bt = jnp.where(up, dot_nt(v, g) * scale, 0.0).astype(BF16)
            acc[2, rows, cols] = dot(bt, q)
            a_t = jnp.where(up, dot_nt(k, q) * scale, 0.0).astype(BF16)
            acc[3, rows, cols] = dot(a_t, g)

    def chunk(i, c):
        poll(i)
        project_near(i)

        @pl.when(i >= 1)
        def _():
            project_far(i - 1)

        @pl.when((i >= 1) & (i < CHUNKS - 1))
        def _():
            attend(i - 1)

        return c

    lax.fori_loop(0, CHUNKS, chunk, 0)
    project_far(CHUNKS - 1)

    chip = me // 2
    offsets = sorted(
        ((dz, dx, dc) for dz in range(4) for dx in range(4) for dc in range(2)),
        key=lambda o: (-o[2], -min(o[0], 4 - o[0]) - min(o[1], 4 - o[1])),
    )[:-1]
    peers = [at_offset(*offset) for offset in offsets]
    gives = []
    give_mixes = []
    for n, (offset, peer) in enumerate(zip(offsets, peers)):
        owned = core if offset[2] == 0 else 1 - core
        gives.append(
            pltpu.make_async_remote_copy(
                src_ref=sbuf.at[owned, peer // 2], dst_ref=rbuf.at[me],
                send_sem=s1.at[n], recv_sem=r1.at[n],
                device_id={"seq": peer}, device_id_type=MESH,
            )
        )
        give_mixes.append(
            pltpu.make_async_remote_copy(
                src_ref=mix.at[peer], dst_ref=fbuf.at[core, chip],
                send_sem=s2.at[n], recv_sem=r2.at[n],
                device_id={"seq": peer}, device_id_type=MESH,
            )
        )

    last = slice(ROWS - ST, ROWS)
    for way in range(2):
        relay(STEPS - 1, way).wait_recv()

    def last_step(kind, states, a, b, parts):
        project(last, parts)
        add_states(CHUNKS - 1, last, states, a, b)
        sbuf[kind] = states[CHUNKS].reshape(CHIPS, SLICE, E).astype(BF16)

    keys = (0, kst, 1, 2, (1, 2))
    queries = (1, qst, 0, 3, (0,))
    for n in range(2):

        @pl.when(core == 1 - n)
        def _():
            last_step(*keys)

        @pl.when(core == n)
        def _():
            last_step(*queries)

        for copy in gives[n * CHIPS : (n + 1) * CHIPS]:
            copy.start()
    rbuf[me] = sbuf[core, chip]

    attend(CHUNKS - 2)

    for copy in gives:
        copy.wait_recv()
    def place_of(c):
        return c + core * (NS - 1 - 2 * c)

    head = chip // (CHIPS // HEADS)
    sums = [rbuf[place_of(c)].astype(F32) for c in range(NS)]
    total = [jnp.zeros((SLICE, E), F32)] * NS
    for b in range(5):
        coef = lw_ref[head, b + 1] * (1.0 / math.sqrt(E * ROWS * 2**b))
        for c in range(NS):
            if c >> b & 1:
                total[c] = total[c] + coef * sums[(c >> b) ^ 1]
        sums = [sums[2 * n] + sums[2 * n + 1] for n in range(len(sums) // 2)]
    for c in range(NS):
        mix[place_of(c)] = total[c].astype(BF16)
    for copy in give_mixes:
        copy.start()
    fbuf[core, chip] = mix[me]
    attend(CHUNKS - 1)

    def later(i, c):
        rows = chunk_rows(i)
        for h in range(HEADS):
            cols = slice(h * E, (h + 1) * E)
            after = ((qst[CHUNKS, cols, :] - qst[i + 1, cols, :]) * local_scale(h)).astype(BF16)
            acc[2, rows, cols] += dot_nt(qkvg[2, rows, cols], after)
            acc[3, rows, cols] += dot(qkvg[1, rows, cols], after)
        return c

    lax.fori_loop(0, CHUNKS - 1, later, 0)

    for j in range(STEPS):
        for way in range(2):
            relay(j, way).wait_send()
    for i in range(CHUNKS):
        for way in range(2):
            own(i, way).wait_send()
    for copy in gives:
        copy.wait_send()
    for copy in give_mixes:
        copy.wait_recv()

    per_head = CHIPS // HEADS
    for h in range(HEADS):
        pair, side = h // 2, h % 2
        span = slice(side * E, (side + 1) * E)
        for part in range(2):
            block = fbuf[part, h * per_head : (h + 1) * per_head].reshape(E, E)
            diag[part, pair, span, span] = block
    for copy in give_mixes:
        copy.wait_send()


def finish_kernel(qkvg, acc, diag, o_ref, gq_ref, gk_ref, gv_ref, buf, sem):
    outs = (o_ref, gq_ref, gk_ref, gv_ref)
    plan = ((0, 0, dot), (3, 0, dot_nt), (2, 1, dot_nt), (1, 1, dot))
    copies = []
    for i in range(CHUNKS):
        rows = slice(i * T, (i + 1) * T)
        for n, (lhs, part, fn) in enumerate(plan):
            for pair in range(2):
                cols = slice(pair * 2 * E, (pair + 1) * 2 * E)
                value = acc[n, rows, cols] + fn(qkvg[lhs, rows, cols], diag[part, pair])
                buf[n, rows, cols] = value.astype(BF16)
            copy = pltpu.make_async_copy(buf.at[n, rows, :], outs[n].at[rows, :], sem.at[n, i])
            copy.start()
            copies.append(copy)
    for copy in copies:
        copy.wait()


def per_device(inputs, w_qkv, level_weight, grad_out):
    place = pltpu.with_memory_space_constraint
    any_spec = pl.BlockSpec(memory_space=pl.ANY)
    vmem = pl.BlockSpec(memory_space=pltpu.VMEM)
    dma = pltpu.SemaphoreType.DMA
    state = pl.pallas_call(
        main_kernel,
        out_shape=(
            pltpu.VMEM((4, ROWS, FEAT), BF16),
            pltpu.VMEM((4, ROWS, FEAT), F32),
            pltpu.VMEM((2, 2, 2 * E, 2 * E), BF16),
        ),
        in_specs=[any_spec] * 4,
        out_specs=(vmem,) * 3,
        scratch_shapes=[
            pltpu.VMEM((ROWS, 4 * FEAT), BF16),
            pltpu.VMEM((3, 4 * FEAT, FEAT), BF16),
            pltpu.VMEM((3, ROWS, FEAT), F32),
            pltpu.VMEM((CHUNKS + 1, FEAT, E), F32),
            pltpu.VMEM((CHUNKS + 1, FEAT, E), F32),
            pltpu.VMEM((2, CHIPS, SLICE, E), BF16),
            pltpu.VMEM((NS, SLICE, E), BF16),
            pltpu.VMEM((NS, SLICE, E), BF16),
            pltpu.VMEM((2, CHIPS, SLICE, E), BF16),
            dma((CHUNKS, 2)),
            dma((CHUNKS, 2)),
            dma((STEPS, 2)),
            dma((STEPS, 2)),
            dma(()),
            dma((4,)),
            dma(()),
            dma((NS,)),
            dma((NS,)),
            dma((NS,)),
            dma((NS,)),
            pltpu.SMEM((HEADS, 6), F32),
            dma(()),
            pltpu.SemaphoreType.REGULAR((4,)),
        ],
        compiler_params=pltpu.CompilerParams(
            collective_id=0, has_side_effects=True, vmem_limit_bytes=36 * 2**20
        ),
        name="gather_and_mix",
    )(*(place(a, pltpu.MemorySpace.HBM) for a in (inputs, w_qkv, level_weight, grad_out)))
    out = jax.ShapeDtypeStruct((ROWS, FEAT), BF16)
    return pl.pallas_call(
        finish_kernel,
        out_shape=(out, out, out, out),
        in_specs=[vmem] * 3,
        out_specs=(any_spec,) * 4,
        scratch_shapes=[pltpu.VMEM((4, ROWS, FEAT), BF16), dma((4, CHUNKS))],
        compiler_params=pltpu.CompilerParams(vmem_limit_bytes=8 * 2**20),
        name="finish",
    )(*(place(a, pltpu.MemorySpace.VMEM) for a in state))


def solution(mesh):
    in_specs = (P("seq", "head"), P(None, None, "head"), P("head", None), P("seq", "head"))
    out_specs = (P("seq", "head"), P("seq", "head"), P("seq", "head"), P("seq", "head"))
    return jax.shard_map(
        per_device, mesh=mesh, in_specs=in_specs, out_specs=out_specs, check_vma=False
    )
```

```python
import functools
import math

import jax
import jax.numpy as jnp
from jax import lax
from jax.experimental import pallas as pl
from jax.experimental.pallas import tpu as pltpu
from jax.sharding import PartitionSpec as P

MESH = pl.DeviceIdType.MESH
NS = 32
NH = 4
ROWS = 1024
FEAT = 512
HEADS = 4
E = 128
STEPS = 8
ST = ROWS // STEPS
HALF = ST // 2
CHUNKS = 4
T = ROWS // CHUNKS
AHEAD = 2
FAR = 3 * FEAT
CHIPS = NS // 2
SLICE = FEAT // CHIPS
F32 = jnp.float32
BF16 = jnp.bfloat16


def dot(a, b):
    return jnp.dot(a, b, preferred_element_type=F32)


def dot_nt(a, b):
    return lax.dot_general(a, b, (((1,), (1,)), ((), ())), preferred_element_type=F32)


def dot_tn(a, b):
    return lax.dot_general(a, b, (((0,), (0,)), ((), ())), preferred_element_type=F32)


def main_kernel(
    x_ref, w_ref, lw_hbm, g_ref,
    qkvg, acc, diag,
    xg, wv, pacc, kst, qst, sbuf, rbuf, mix, fbuf,
    own_s, own_r, rel_s, rel_r, loc_sem, w_sem, g_sem, s1, r1, s2, r2, lw_ref, lw_sem, word,
):
    me = lax.axis_index("seq")
    y = lax.axis_index("head")
    right = lax.rem(y + 1, NH)
    left = lax.rem(y + 3, NH)
    far = lax.rem(y + 2, NH)

    sources = (y, left, right, far)
    w_copies = [
        pltpu.make_async_copy(
            w_ref.at[:, pl.ds(pl.multiple_of(src * FEAT, FEAT), FEAT), :],
            wv.at[:, slot * FEAT : (slot + 1) * FEAT, :],
            w_sem.at[slot],
        )
        for slot, src in enumerate(sources)
    ]
    x_copy = pltpu.make_async_copy(x_ref, xg.at[:, 0:FEAT], loc_sem)
    g_copy = pltpu.make_async_copy(g_ref, qkvg.at[3], g_sem)
    lw_copy = pltpu.make_async_copy(lw_hbm, lw_ref, lw_sem)

    core = lax.rem(me, 2)
    along_x = lax.rem(me // 2, 4)
    along_z = me // 8

    def at_offset(dz, dx, dc):
        z = lax.rem(along_z + dz, 4) * 8
        x = lax.rem(along_x + dx, 4) * 2
        return z + x + (core if dc == 0 else 1 - core)

    x_peers = [at_offset(0, d, 0) for d in (1, 3)]
    z_peers = [at_offset(d, 0, 0) for d in (1, 3)]
    partner = at_offset(0, 0, 1)
    barrier = pltpu.get_barrier_semaphore()

    def signal(sem, axis, device):
        pl.semaphore_signal(sem, inc=1, device_id={axis: device}, device_id_type=MESH)

    for device in (left, right):
        signal(barrier, "head", device)
    for device in (*x_peers, *z_peers, partner):
        signal(barrier, "seq", device)
    x_copy.start()
    for copy in w_copies:
        copy.start()
    g_copy.start()
    lw_copy.start()
    pl.semaphore_wait(barrier, 7)

    def own(i, way):
        rows = pl.ds(pl.multiple_of(i * T, T), T)
        return pltpu.make_async_remote_copy(
            src_ref=x_ref.at[rows, :],
            dst_ref=xg.at[rows, (way + 1) * FEAT : (way + 2) * FEAT],
            send_sem=own_s.at[i, way],
            recv_sem=own_r.at[i, way],
            device_id={"head": right if way == 0 else left},
            device_id_type=MESH,
        )

    def relay(j, way):
        rows = pl.ds(pl.multiple_of(j * ST + way * HALF, HALF), HALF)
        return pltpu.make_async_remote_copy(
            src_ref=xg.at[rows, (way + 1) * FEAT : (way + 2) * FEAT],
            dst_ref=xg.at[rows, FAR : FAR + FEAT],
            send_sem=rel_s.at[j, way],
            recv_sem=rel_r.at[j, way],
            device_id={"head": right if way == 0 else left},
            device_id_type=MESH,
        )

    def relay_chunk(i, way):
        rows = pl.ds(pl.multiple_of(i * T + way * ST, ST), ST)
        return pltpu.make_async_remote_copy(
            src_ref=xg.at[rows, (way + 1) * FEAT : (way + 2) * FEAT],
            dst_ref=xg.at[rows, FAR : FAR + FEAT],
            send_sem=rel_s.at[2 * i, way],
            recv_sem=rel_r.at[2 * i, way],
            device_id={"head": right if way == 0 else left},
            device_id_type=MESH,
        )

    def start_own(i):
        for way in range(2):
            own(i, way).start()

    for i in range(AHEAD):
        start_own(i)
    for n, peers in enumerate((x_peers, z_peers, z_peers, [partner])):
        for device in peers:
            signal(word.at[n], "seq", device)
        pl.semaphore_wait(word.at[n], len(peers))
    diag[...] = jnp.zeros_like(diag)
    kst[0] = jnp.zeros((FEAT, E), F32)
    qst[0] = jnp.zeros((FEAT, E), F32)
    x_copy.wait()
    for copy in w_copies:
        copy.wait()
    g_copy.wait()
    lw_copy.wait()

    def poll(i):
        for way in range(2):
            own(i, way).wait_recv()

            @pl.when(i < CHUNKS - 1)
            def _():
                relay_chunk(i, way).start()

            @pl.when(i == CHUNKS - 1)
            def _():
                for step in range(T // ST):
                    relay(i * (T // ST) + step, way).start()

        @pl.when(i + AHEAD < CHUNKS)
        def _():
            start_own(i + AHEAD)

    def chunk_rows(i):
        return pl.ds(pl.multiple_of(i * T, T), T)

    def project_near(i):
        rows = chunk_rows(i)
        for p in range(3):
            pacc[p, rows, :] = dot(xg[rows, 0:FAR], wv[p, 0:FAR, :])

    def project_far(i):
        for h in range(HEADS):
            cols = slice(h * E, (h + 1) * E)
            kst[i + 1, cols, :] = kst[i, cols, :]
            qst[i + 1, cols, :] = qst[i, cols, :]

        @pl.when(i < CHUNKS - 1)
        def _():
            for way in range(2):
                relay_chunk(i, way).wait_recv()

        @pl.when(i == CHUNKS - 1)
        def _():
            for way in range(2):
                relay(2 * i, way).wait_recv()

        far_step(i, 0)

        @pl.when(i < CHUNKS - 1)
        def _():
            far_step(i, 1)

    def far_step(i, step):
        rows = pl.ds(pl.multiple_of(i * T + step * ST, ST), ST)
        project(rows, (0, 1, 2))
        add_states(i, rows, kst, 1, 2)
        add_states(i, rows, qst, 0, 3)

    def project(rows, parts):
        for p in parts:
            full = pacc[p, rows, :] + dot(xg[rows, FAR : FAR + FEAT], wv[p, FAR : FAR + FEAT, :])
            qkvg[p, rows, :] = full.astype(BF16)

    def add_states(i, rows, states, a, b):
        for h in range(HEADS):
            cols = slice(h * E, (h + 1) * E)
            states[i + 1, cols, :] += dot_tn(qkvg[a, rows, cols], qkvg[b, rows, cols])

    def local_scale(h):
        return lw_ref[h, 0] * (1.0 / math.sqrt(E * ROWS))

    def attend(i):
        rows = chunk_rows(i)
        at = lax.broadcasted_iota(jnp.int32, (T, T), 0)
        to = lax.broadcasted_iota(jnp.int32, (T, T), 1)
        for h in range(HEADS):
            cols = slice(h * E, (h + 1) * E)
            scale = local_scale(h)
            q, k, v, g = (qkvg[n, rows, cols] for n in range(4))
            before = (kst[i, cols, :] * scale).astype(BF16)
            low = at >= to
            up = at <= to
            a = jnp.where(low, dot_nt(q, k) * scale, 0.0).astype(BF16)
            acc[0, rows, cols] = dot(a, v) + dot(q, before)
            b = jnp.where(low, dot_nt(g, v) * scale, 0.0).astype(BF16)
            acc[1, rows, cols] = dot(b, k) + dot_nt(g, before)
            bt = jnp.where(up, dot_nt(v, g) * scale, 0.0).astype(BF16)
            acc[2, rows, cols] = dot(bt, q)
            a_t = jnp.where(up, dot_nt(k, q) * scale, 0.0).astype(BF16)
            acc[3, rows, cols] = dot(a_t, g)

    def chunk(i, c):
        poll(i)
        project_near(i)

        @pl.when(i >= 1)
        def _():
            project_far(i - 1)

        @pl.when(i == 1)
        def _():
            attend(i - 1)

        return c

    lax.fori_loop(0, CHUNKS, chunk, 0)
    project_far(CHUNKS - 1)

    chip = me // 2
    offsets = sorted(
        ((dz, dx, dc) for dz in range(4) for dx in range(4) for dc in range(2)),
        key=lambda o: (-o[2], -min(o[0], 4 - o[0]) - min(o[1], 4 - o[1])),
    )[:-1]
    peers = [at_offset(*offset) for offset in offsets]
    gives = []
    give_mixes = []
    for n, (offset, peer) in enumerate(zip(offsets, peers)):
        owned = core if offset[2] == 0 else 1 - core
        gives.append(
            pltpu.make_async_remote_copy(
                src_ref=sbuf.at[owned, peer // 2], dst_ref=rbuf.at[me],
                send_sem=s1.at[n], recv_sem=r1.at[n],
                device_id={"seq": peer}, device_id_type=MESH,
            )
        )
        give_mixes.append(
            pltpu.make_async_remote_copy(
                src_ref=mix.at[peer], dst_ref=fbuf.at[core, chip],
                send_sem=s2.at[n], recv_sem=r2.at[n],
                device_id={"seq": peer}, device_id_type=MESH,
            )
        )

    last = slice(ROWS - ST, ROWS)
    for way in range(2):
        relay(STEPS - 1, way).wait_recv()

    def last_step(kind, states, a, b, parts):
        project(last, parts)
        add_states(CHUNKS - 1, last, states, a, b)
        sbuf[kind] = states[CHUNKS].reshape(CHIPS, SLICE, E).astype(BF16)

    keys = (0, kst, 1, 2, (1, 2))
    queries = (1, qst, 0, 3, (0,))
    for n in range(2):

        @pl.when(core == 1 - n)
        def _():
            last_step(*keys)

        @pl.when(core == n)
        def _():
            last_step(*queries)

        for copy in gives[n * CHIPS : (n + 1) * CHIPS]:
            copy.start()
    rbuf[me] = sbuf[core, chip]

    lax.fori_loop(1, CHUNKS - 1, lambda i, c: (attend(i), c)[1], 0)

    for copy in gives:
        copy.wait_recv()
    def place_of(c):
        return c + core * (NS - 1 - 2 * c)

    head = chip // (CHIPS // HEADS)
    sums = [rbuf[place_of(c)].astype(F32) for c in range(NS)]
    total = [jnp.zeros((SLICE, E), F32)] * NS
    for b in range(5):
        coef = lw_ref[head, b + 1] * (1.0 / math.sqrt(E * ROWS * 2**b))
        for c in range(NS):
            if c >> b & 1:
                total[c] = total[c] + coef * sums[(c >> b) ^ 1]
        sums = [sums[2 * n] + sums[2 * n + 1] for n in range(len(sums) // 2)]
    for c in range(NS):
        mix[place_of(c)] = total[c].astype(BF16)
    for copy in give_mixes:
        copy.start()
    fbuf[core, chip] = mix[me]
    attend(CHUNKS - 1)

    def later(i, c):
        rows = chunk_rows(i)
        for h in range(HEADS):
            cols = slice(h * E, (h + 1) * E)
            after = ((qst[CHUNKS, cols, :] - qst[i + 1, cols, :]) * local_scale(h)).astype(BF16)
            acc[2, rows, cols] += dot_nt(qkvg[2, rows, cols], after)
            acc[3, rows, cols] += dot(qkvg[1, rows, cols], after)
        return c

    lax.fori_loop(0, CHUNKS - 1, later, 0)

    for way in range(2):
        for i in range(CHUNKS - 1):
            relay_chunk(i, way).wait_send()
        for j in range(STEPS - 2, STEPS):
            relay(j, way).wait_send()
    for i in range(CHUNKS):
        for way in range(2):
            own(i, way).wait_send()
    for copy in gives:
        copy.wait_send()
    for copy in give_mixes:
        copy.wait_recv()

    per_head = CHIPS // HEADS
    for h in range(HEADS):
        pair, side = h // 2, h % 2
        span = slice(side * E, (side + 1) * E)
        for part in range(2):
            block = fbuf[part, h * per_head : (h + 1) * per_head].reshape(E, E)
            diag[part, pair, span, span] = block
    for copy in give_mixes:
        copy.wait_send()


def finish_kernel(qkvg, acc, diag, o_ref, gq_ref, gk_ref, gv_ref, buf, sem):
    outs = (o_ref, gq_ref, gk_ref, gv_ref)
    plan = ((0, 0, dot), (3, 0, dot_nt), (2, 1, dot_nt), (1, 1, dot))
    copies = []
    for i in range(CHUNKS):
        rows = slice(i * T, (i + 1) * T)
        for n, (lhs, part, fn) in enumerate(plan):
            for pair in range(2):
                cols = slice(pair * 2 * E, (pair + 1) * 2 * E)
                value = acc[n, rows, cols] + fn(qkvg[lhs, rows, cols], diag[part, pair])
                buf[n, rows, cols] = value.astype(BF16)
            copy = pltpu.make_async_copy(buf.at[n, rows, :], outs[n].at[rows, :], sem.at[n, i])
            copy.start()
            copies.append(copy)
    for copy in copies:
        copy.wait()


def per_device(inputs, w_qkv, level_weight, grad_out):
    place = pltpu.with_memory_space_constraint
    any_spec = pl.BlockSpec(memory_space=pl.ANY)
    vmem = pl.BlockSpec(memory_space=pltpu.VMEM)
    dma = pltpu.SemaphoreType.DMA
    state = pl.pallas_call(
        main_kernel,
        out_shape=(
            pltpu.VMEM((4, ROWS, FEAT), BF16),
            pltpu.VMEM((4, ROWS, FEAT), F32),
            pltpu.VMEM((2, 2, 2 * E, 2 * E), BF16),
        ),
        in_specs=[any_spec] * 4,
        out_specs=(vmem,) * 3,
        scratch_shapes=[
            pltpu.VMEM((ROWS, 4 * FEAT), BF16),
            pltpu.VMEM((3, 4 * FEAT, FEAT), BF16),
            pltpu.VMEM((3, ROWS, FEAT), F32),
            pltpu.VMEM((CHUNKS + 1, FEAT, E), F32),
            pltpu.VMEM((CHUNKS + 1, FEAT, E), F32),
            pltpu.VMEM((2, CHIPS, SLICE, E), BF16),
            pltpu.VMEM((NS, SLICE, E), BF16),
            pltpu.VMEM((NS, SLICE, E), BF16),
            pltpu.VMEM((2, CHIPS, SLICE, E), BF16),
            dma((CHUNKS, 2)),
            dma((CHUNKS, 2)),
            dma((STEPS, 2)),
            dma((STEPS, 2)),
            dma(()),
            dma((4,)),
            dma(()),
            dma((NS,)),
            dma((NS,)),
            dma((NS,)),
            dma((NS,)),
            pltpu.SMEM((HEADS, 6), F32),
            dma(()),
            pltpu.SemaphoreType.REGULAR((4,)),
        ],
        compiler_params=pltpu.CompilerParams(
            collective_id=0, has_side_effects=True, vmem_limit_bytes=36 * 2**20
        ),
        name="gather_and_mix",
    )(*(place(a, pltpu.MemorySpace.HBM) for a in (inputs, w_qkv, level_weight, grad_out)))
    out = jax.ShapeDtypeStruct((ROWS, FEAT), BF16)
    return pl.pallas_call(
        finish_kernel,
        out_shape=(out, out, out, out),
        in_specs=[vmem] * 3,
        out_specs=(any_spec,) * 4,
        scratch_shapes=[pltpu.VMEM((4, ROWS, FEAT), BF16), dma((4, CHUNKS))],
        compiler_params=pltpu.CompilerParams(vmem_limit_bytes=8 * 2**20),
        name="finish",
    )(*(place(a, pltpu.MemorySpace.VMEM) for a in state))


def solution(mesh):
    in_specs = (P("seq", "head"), P(None, None, "head"), P("head", None), P("seq", "head"))
    out_specs = (P("seq", "head"), P("seq", "head"), P("seq", "head"), P("seq", "head"))
    return jax.shard_map(
        per_device, mesh=mesh, in_specs=in_specs, out_specs=out_specs, check_vma=False
    )
```
